512 devices in a mesh: row: 32 (over z, y_lo, core), col: 16 (over x, y_hi).
Axes of the slice: x: 4, y: 8 (y_hi: 4, y_lo: 2; y = y_hi * 2 + y_lo), z: 8, core: 2. Of those that a mesh axis runs over, the one named last changes fastest.
Arguments:
- inputs: float32 [2048, 8192], P('col', 'row'), may hold values from -6 to 6
- lang_ids: int32 [2048], P('row'), may hold values from 0 to 7
- group_table: int32 [8, 192], P(None, 'col'), may hold values 0 or 1
- cotangent: float32 [2048, 24576], P('row', 'col'), may hold values from -6 to 6
- weight: float32 [8192, 24576], P('row', 'col'), may hold values from -0.0390625 to 0.0390625
Outputs:
- weight_grad: float32 [8192, 24576], P('row', 'col')
- input_grad: float32 [2048, 8192], P('col', 'row')
The draws below stay inside these ranges and needn't reach their ends.
All inputs are finite; a program needn't handle non-finite values. No bound on the sum of `group_table` on one device may be relied on, other than what follows from the above.
Results may differ from the reference program's by a relative error of at most 0.000092.
Values sent between devices are 32-bit elements; how exact they have to be, the bound alone decides.
A program may use at most 64 MiB of HBM per device.

```python
import jax
import jax.numpy as jnp
from jax import lax

D = 8192
FF = 24576
GROUP_W = 128
LANGS = 8
TOKENS = 2048
GROUPS = 192


def plant(entries, stream_key, least, top_value):
    extent = entries.shape
    spot = [jax.random.randint(jax.random.fold_in(stream_key, axis), (), 0, extent[axis]) for axis in range(len(extent))]
    entries = entries.at[tuple(spot)].set(least)
    longest = extent.index(max(extent))
    spot[longest] = (spot[longest] + 1) % extent[longest]
    return entries.at[tuple(spot)].set(top_value)


def raised(drawn, stream_key, source, target, blocks, factor):
    def block_of(axis_at):
        return (jnp.arange(drawn.shape[axis_at]) // (drawn.shape[axis_at] // blocks)).reshape((-1,) + (1,) * (drawn.ndim - 1 - axis_at))

    near = jax.random.permutation(stream_key, blocks)[block_of(target)]
    other_side = (block_of(target) + blocks // 2) % blocks
    return jnp.where((block_of(source) == near) | (block_of(source) == other_side), factor * drawn, drawn)


def steps_of(rng, shape, pieces, smallest, high):
    loudness = 1.0
    for dim, parts in pieces:
        steps = jax.random.uniform(jax.random.fold_in(jax.random.fold_in(rng, 6), dim), (parts,), jnp.float32, smallest / len(pieces), high / len(pieces))
        loudness = loudness * jnp.repeat(jnp.exp(steps), shape[dim] // parts).reshape((-1,) + (1,) * (len(shape) - 1 - dim))
    return loudness


def noise(stream_key, dims, spread, bound, shards=(), dtype=jnp.bfloat16):
    drawn = spread * jax.random.normal(stream_key, dims, jnp.float32)
    if shards:
        drawn = drawn * steps_of(stream_key, dims, shards, -0.22, 0.18)
    return jnp.clip(drawn, -bound, bound).astype(dtype)


def heavy_noise(stream_key, dims, spread, limit, split, heavy, held_as=jnp.bfloat16):
    entries = spread * jax.random.normal(stream_key, dims, jnp.float32)
    if split:
        entries = entries * steps_of(stream_key, dims, split, -0.22, 0.18)
    return jnp.clip(raised(entries, jax.random.fold_in(stream_key, 3), *heavy), -limit, limit).astype(held_as)


def setup_inputs(seed: int = 0) -> dict:
    streams_of = jax.random.split(jax.random.key(seed), 6)
    inputs = noise(streams_of[0], (TOKENS, D), 1.0, 6.0, ((0, 16), (1, 32)), jnp.float32)
    lang_ids = plant(jax.random.randint(streams_of[1], (TOKENS,), 0, LANGS), jax.random.fold_in(streams_of[1], 1), 0, LANGS - 1).astype(jnp.int32)
    group_table = plant((jax.random.randint(streams_of[2], (LANGS, GROUPS), 0, 2) < 1).astype(jnp.int32), jax.random.fold_in(streams_of[2], 1), 0, 1)
    cotangent = heavy_noise(streams_of[3], (TOKENS, FF), 1.0, 6.0, ((0, 32), (1, 16)), (1, 0, 32, 2.75), jnp.float32)
    weight = noise(streams_of[4], (D, FF), FF ** -0.5, 0.0390625, ((0, 32), (1, 16)), jnp.float32)
    return dict(inputs=inputs, lang_ids=lang_ids, group_table=group_table, cotangent=cotangent, weight=weight)


def reference(inputs, lang_ids, group_table, cotangent, weight):
    table_rows = group_table[lang_ids].astype(jnp.float32)
    mask_full = jnp.repeat(table_rows, GROUP_W, axis=1)
    masked = cotangent * mask_full
    weight_grad = jnp.dot(inputs.T, masked, preferred_element_type=jnp.float32, precision=lax.Precision.HIGHEST)
    input_grad = jnp.dot(masked, weight.T, preferred_element_type=jnp.float32, precision=lax.Precision.HIGHEST)
    return weight_grad, input_grad
```

```python
import functools

import jax
import jax.numpy as jnp
from jax import lax
from jax.experimental import pallas as pl
from jax.experimental.pallas import tpu as pltpu
from jax.sharding import PartitionSpec as P

MESH = pl.DeviceIdType.MESH
BF16 = jnp.bfloat16
F32 = jnp.float32

STAGES = 4
ACROSS = 512
PIECE = 512
NZ, NX, NH = 8, 4, 4


def dot(a, b, dims):
    return lax.dot_general(a, b, (dims, ((), ())), preferred_element_type=F32)


def split(v):
    hi = v.astype(BF16)
    return hi, (v - hi.astype(F32)).astype(BF16)


def kernel(
    lang_hbm, table_hbm, g_hbm, x_hbm, w_hbm,
    dw_hbm, dx_hbm,
    lang, table, graw, w, gbuf, xbuf, pbuf, xrecv, ysum, yrecv, dxo,
    ghi, glo, whi, wlo, xthi, xtlo, dw,
    load_sem, zr, yr, kr, xh, xx, rx, ry, zs, ys, ks, xhs, xxs, rxs, rys, out_sem,
):
    S = gbuf.shape[0]
    T = gbuf.shape[4]
    F = gbuf.shape[5]
    M = 4 * NZ * T
    row, col = lax.axis_index("row"), lax.axis_index("col")
    z, l, k = row // 4, (row // 2) % 2, row % 2
    x, h = col // NH, col % NH
    ol, ok = 1 - l, 1 - k
    sg = 1 - 2 * k

    def at_row(dz, li, ki):
        return (((z + dz + NZ) % NZ) * 4 + li * 2 + ki, col)

    z1, z2 = at_row(sg, l, k), at_row(-sg, l, k)
    ypair, kpair = at_row(0, ol, k), at_row(0, l, ok)
    xdev = [(row, ((x + d) % NX) * NH + h) for d in (1, 3, 2)]
    hdev = [(row, x * NH + (h + d) % NH) for d in (1, 3, 2)]

    barrier = pltpu.get_barrier_semaphore()
    partners = [z1, z2, ypair, kpair] + xdev + hdev
    for p in partners:
        pl.semaphore_signal(barrier, inc=1, device_id=p, device_id_type=MESH)

    loads = [
        pltpu.make_async_copy(a, b, load_sem.at[i])
        for i, (a, b) in enumerate(
            ((lang_hbm, lang), (table_hbm, table), (g_hbm, graw), (w_hbm, w))
        )
    ]
    for c in loads:
        c.start()
    own_x = [pltpu.make_async_copy(x_hbm.at[i], xbuf.at[:, i, col], load_sem.at[4 + i]) for i in (0, 1)]
    for c in own_x:
        c.start()
    for c in loads[:3]:
        c.wait()
    labels = lax.broadcasted_iota(jnp.int32, (8, lang.shape[1]), 0)
    onehot = jnp.where(labels == lang[...], 1.0, 0.0).astype(F32)
    tab = table[...].astype(F32)
    wide = jnp.concatenate(
        [jnp.broadcast_to(tab[:, g : g + 1], (8, F // tab.shape[1])) for g in range(tab.shape[1])], axis=1
    )
    mask = dot(onehot, wide, ((0,), (0,)))
    masked = graw[...] * mask
    gbuf[:, k, z, l] = masked.reshape(S, T, F)
    for c in own_x:
        c.wait()
    pl.semaphore_wait(barrier, len(partners))

    def remote(src, dst, ssem, rsem, dev):
        return pltpu.make_async_remote_copy(
            src_ref=src, dst_ref=dst, send_sem=ssem, recv_sem=rsem, device_id=dev, device_id_type=MESH
        )

    def zsrc(dirn, d):
        return (z - sg * d + 2 * NZ) % NZ if dirn == 0 else (z + sg * d + 2 * NZ) % NZ

    reach = (NZ // 2, NZ // 2 - 1)

    def zcopy(s, dirn, d, which):
        zi = zsrc(dirn, d)
        ref = gbuf.at[s, k, zi, l] if which == 0 else gbuf.at[s, k, zi, ol, :, pl.ds(ACROSS, F - ACROSS)]
        return remote(ref, ref, zs.at[which], zr.at[s, dirn, d, which], z1 if dirn == 0 else z2)

    def zarrived(s, dirn, d, which):
        zi = zsrc(dirn, d)
        ref = gbuf.at[s, k, zi, l] if which == 0 else gbuf.at[s, k, zi, ol, :, pl.ds(ACROSS, F - ACROSS)]
        remote(ref, ref, zs.at[which], zr.at[s, dirn, d - 1, which], z1).wait_recv()

    def ycopy(s, dirn, d, to_me=False):
        li = ol if to_me else l
        zi = zsrc(dirn, d)
        ref = gbuf.at[s, k, zi, li] if d == 0 else gbuf.at[s, k, zi, li, :, pl.ds(0, ACROSS)]
        return remote(ref, ref, ys.at[0 if d == 0 else 1], yr.at[s, 0 if d == 0 else d + 4 * dirn], ypair)

    def kcopy(s, zi, ki):
        ref = gbuf.at[s, ki, zi]
        return remote(ref, ref, ks, kr.at[s, zi], kpair)

    def zsend(s, d, which):
        for dirn in (0, 1):
            if d < reach[dirn]:
                zcopy(s, dirn, d, which).start()

    def handle(s, d):
        for dirn in (0, 1):
            if d <= reach[dirn]:
                for which in (0, 1):
                    zarrived(s, dirn, d, which)
                    if d < reach[dirn]:
                        zcopy(s, dirn, d, which).start()
                ycopy(s, dirn, d).start()

    def kfin(s, d):
        for dirn in (0, 1):
            if d <= reach[dirn]:
                ycopy(s, dirn, d, True).wait_recv()
                kcopy(s, zsrc(dirn, d), k).start()

    def xh_copy(s, j):
        ref = xbuf.at[s, :, col]
        return remote(ref, ref, xhs, xh.at[s, j], hdev[j])

    def xx_copy(s, j):
        ref = xbuf.at[s, :, pl.ds(x * NH, NH)]
        return remote(ref, ref, xxs, xx.at[s, j], xdev[j])

    def rx_copy(s, j):
        xd = (x + (1, 3, 2)[j]) % NX
        return remote(pbuf.at[s, :, pl.ds(xd * NH, NH)], xrecv.at[s, j], rxs, rx.at[s, j], xdev[j])

    def ry_copy(s, j):
        hd = (h + (1, 3, 2)[j]) % NH
        return remote(ysum.at[s, :, hd], yrecv.at[s, j], rys, ry.at[s, j], hdev[j])

    def when(lo, i, hi):
        return pl.when(jnp.logical_and(i >= lo, i < hi))

    ycopy(0, 0, 0).start()
    zsend(0, 0, 0)
    for j in range(3):
        xh_copy(0, j).start()
    dw[...] = jnp.zeros_like(dw)
    loads[3].wait()
    for q in range(F // PIECE):
        sl = pl.ds(q * PIECE, PIECE)
        whi[:, sl], wlo[:, sl] = split(w[:, sl])

    def ppiece(s, q):
        sl = pl.ds(q * PIECE, PIECE)
        hi, lo = split(gbuf[s, :, :, :, :, sl].reshape(M, PIECE))
        ghi[:, sl] = hi
        glo[:, sl] = lo
        nt = ((1,), (1,))
        part = dot(hi, whi[:, sl], nt) + dot(lo, whi[:, sl], nt) + dot(hi, wlo[:, sl], nt)
        part = part.reshape(pbuf.shape[1:])
        if q == 0:
            pbuf[s] = part
        else:
            pbuf[s] += part

    def xprep(s):
        xt = xbuf[s].reshape(M, xbuf.shape[-1]).T
        xthi[...], xtlo[...] = split(xt)

    def wpiece(q):
        sl = pl.ds(q * PIECE, PIECE)
        nn = ((1,), (0,))
        dw[:, sl] += (
            dot(xthi[...], ghi[:, sl], nn) + dot(xtlo[...], ghi[:, sl], nn) + dot(xthi[...], glo[:, sl], nn)
        )

    def body(i, carry):
        @pl.when(i + 1 < S)
        def _():
            ycopy(i + 1, 0, 0).start()
            for j in range(3):
                xh_copy(i + 1, j).start()

        @when(2, i, S + 2)
        def _():
            kfin(i - 2, 3)
            handle(i - 2, 4)

        @pl.when(i < S)
        def _():
            ycopy(i, 0, 0, True).wait_recv()
            zsend(i, 0, 1)
            kcopy(i, z, k).start()

        @when(1, i, S + 1)
        def _():
            handle(i - 1, 2)

        @pl.when(i + 1 < S)
        def _():
            zsend(i + 1, 0, 0)

        @pl.when(i < S)
        def _():
            for j in range(3):
                xh_copy(i, j).wait_recv()
            for j in range(3):
                xx_copy(i, j).start()

        @when(2, i, S + 2)
        def _():
            s = i - 2
            kfin(s, 4)
            for zi in range(NZ):
                kcopy(s, zi, ok).wait_recv()
            for q in range(F // PIECE):
                ppiece(s, q)

        @pl.when(i < S)
        def _():
            handle(i, 1)

        @when(1, i, S + 1)
        def _():
            kfin(i - 1, 2)

        @when(2, i, S + 2)
        def _():
            s = i - 2
            for j in range(3):
                rx_copy(s, j).start()
            for j in range(3):
                xx_copy(s, j).wait_recv()
            xprep(s)
            for q in range(F // PIECE):
                wpiece(q)

        @pl.when(i == S + 1)
        def _():
            pltpu.make_async_copy(dw, dw_hbm, out_sem.at[0]).start()

        @when(1, i, S + 1)
        def _():
            handle(i - 1, 3)

        @pl.when(i < S)
        def _():
            kfin(i, 1)

        @when(4, i, S + 4)
        def _():
            s = i - 4
            for j in range(3):
                ry_copy(s, j).wait_recv()
            dxo[:, s] = (ysum[s, :, h] + yrecv[s, 0]) + (yrecv[s, 1] + yrecv[s, 2])

        @when(3, i, S + 3)
        def _():
            s = i - 3
            for j in range(3):
                rx_copy(s, j).wait_recv()
            ysum[s] = (pbuf[s, :, pl.ds(x * NH, NH)] + xrecv[s, 0]) + (xrecv[s, 1] + xrecv[s, 2])
            for j in range(3):
                ry_copy(s, j).start()

        return carry

    lax.fori_loop(0, S + 4, body, 0)
    pltpu.make_async_copy(dxo, dx_hbm, out_sem.at[1]).start()

    def drain(ref, sem):
        remote(ref, ref, sem, sem, z1).wait_send()

    far = NZ - 1
    drain(gbuf.at[:, 0, pl.ds(0, far), 0], zs.at[0])
    drain(gbuf.at[:, 0, pl.ds(0, far), 0, :, pl.ds(ACROSS, F - ACROSS)], zs.at[1])
    drain(gbuf.at[:, 0, 0, 0], ys.at[0])
    drain(gbuf.at[:, 0, pl.ds(0, far), 0, :, pl.ds(0, ACROSS)], ys.at[1])
    drain(gbuf.at[:, 0], ks)
    drain(xbuf.at[:, :, pl.ds(0, 3)], xhs)
    drain(xbuf.at[:, :, pl.ds(0, 3 * NH)], xxs)
    drain(xrecv, rxs)
    drain(yrecv, rys)
    pltpu.make_async_copy(dw, dw_hbm, out_sem.at[0]).wait()
    pltpu.make_async_copy(dxo, dx_hbm, out_sem.at[1]).wait()


def per_device(inputs, lang_ids, group_table, cotangent, weight):
    S = STAGES
    tokens, F = cotangent.shape
    D = inputs.shape[1]
    T = tokens // S
    M = 4 * NZ * T
    xin = inputs.reshape(2, S, T, D)
    anywhere = pl.BlockSpec(memory_space=pl.ANY)
    dma = pltpu.SemaphoreType.DMA
    dw, dx = pl.pallas_call(
        kernel,
        name="backward",
        out_shape=(
            jax.ShapeDtypeStruct((D, F), F32),
            jax.ShapeDtypeStruct((2, S, T, D), F32),
        ),
        in_specs=[anywhere] * 5,
        out_specs=(anywhere, anywhere),
        scratch_shapes=[
            pltpu.VMEM((1, tokens), jnp.int32),
            pltpu.VMEM(group_table.shape, jnp.int32),
            pltpu.VMEM((tokens, F), F32),
            pltpu.VMEM((D, F), F32),
            pltpu.VMEM((S, 2, NZ, 2, T, F), F32),
            pltpu.VMEM((S, 2, NX * NH, T, D), F32),
            pltpu.VMEM((S, 2, NX * NH, T, D), F32),
            pltpu.VMEM((S, 3, 2, NH, T, D), F32),
            pltpu.VMEM((S, 2, NH, T, D), F32),
            pltpu.VMEM((S, 3, 2, T, D), F32),
            pltpu.VMEM((2, S, T, D), F32),
            pltpu.VMEM((M, F), BF16),
            pltpu.VMEM((M, F), BF16),
            pltpu.VMEM((D, F), BF16),
            pltpu.VMEM((D, F), BF16),
            pltpu.VMEM((D, M), BF16),
            pltpu.VMEM((D, M), BF16),
            pltpu.VMEM((D, F), F32),
            dma((6,)),
            dma((S, 2, NZ // 2, 2)),
            dma((S, NZ)),
            dma((S, NZ)),
            dma((S, 3)),
            dma((S, 3)),
            dma((S, 3)),
            dma((S, 3)),
            dma((2,)),
            dma((2,)),
            dma,
            dma,
            dma,
            dma,
            dma,
            dma((2,)),
        ],
        compiler_params=pltpu.CompilerParams(
            collective_id=0, has_side_effects=True, vmem_limit_bytes=60 * 2**20
        ),
    )(lang_ids.reshape(1, tokens), group_table, cotangent, xin, weight)
    return dw, dx.reshape(2 * tokens, D)


def solution(mesh):
    placed = (P("col", "row"), P("row"), P(None, "col"), P("row", "col"), P("row", "col"))
    return jax.shard_map(
        per_device,
        mesh=mesh,
        in_specs=placed,
        out_specs=(P("row", "col"), P("col", "row")),
        check_vma=False,
    )
```
